32 devices in a mesh: group: 4 (over y, x), seq: 8 (over z, core).
Axes of the slice: x: 2, y: 2, z: 4, core: 2. Of those that a mesh axis runs over, the one named last changes fastest.
Arguments:
- tokens: bfloat16 [32, 2048, 2048], P('group', 'seq'), may hold values from -6 to 6
- image_keys: bfloat16 [32, 256, 2048], P('group', 'seq'), may hold values from -256 to 256
- image_values: bfloat16 [32, 256, 2048], P('group', 'seq'), may hold values from -18 to 18
- text_len: int32 [32], replicated, may hold values from 1 to 2048
- image_len: int32 [32], replicated, may hold values from 1 to 256
- counts: int32 [6], replicated, may hold values from 1 to 4, as said below
- old_group: int32 [6], replicated, may hold values from 0 to 3, as said below
- new_group: int32 [6], replicated, may hold values from 0 to 3, as said below
- w_query: bfloat16 [2048, 2048], replicated, may hold values from -0.125 to 0.125
- w_out: bfloat16 [2048, 2048], replicated, may hold values from -0.125 to 0.125
Outputs:
- layer_out: bfloat16 [32, 2048, 2048], P('group', 'seq')
The draws below stay inside these ranges and needn't reach their ends.
Inputs may be any that keep to these rules, and one draw needn't show every extreme that they name: `counts`: every task has at most 4 samples, and some task has exactly 4. `old_group`: each group is the old group of at most two tasks, and no two tasks share both their old group and their new group, so at most 4 samples go from one old group to one new group. `new_group`: each group is the new group of at most two tasks.
All inputs are finite; a program needn't handle non-finite values.
Results may differ from the reference program's by a relative error of at most 0.011.
Values may be sent and summed in bfloat16 or wider, within the bound.
A program may use at most 128 MiB of HBM per device.

```python
import jax
import jax.numpy as jnp
from jax import lax

D = 2048
HEADS = 16
HEAD_DIM = 128
SAMPLE = 2048
IMG = 256
TASKS = 6
SLOTS = 8
HALF = 4
HH = 2048
TOTAL_SLOTS = 32
N_GROUP = 4


def draw_image_keys(key, part):
    drawn = jax.random.normal(jax.random.fold_in(key, 31), (N_GROUP * SLOTS, IMG, HEADS * HEAD_DIM), jnp.float32)
    drawn = jnp.clip(drawn, -6.0, 6.0)
    return drawn.astype(jnp.bfloat16)


def draw_counts(key, part):
    lowered = jax.random.randint(jax.random.fold_in(key, 5), (TASKS,), 0, 4, dtype=jnp.int32)
    smaller = jnp.maximum(HALF - 1, 1)
    drawn_counts = jnp.where(lowered == 0, smaller, HALF)
    chosen_task = jax.random.randint(jax.random.fold_in(key, 6), (), 0, TASKS, dtype=jnp.int32)
    task_ids = jnp.arange(TASKS, dtype=jnp.int32)
    return jnp.where(task_ids == chosen_task, HALF, drawn_counts).astype(jnp.int32)


def draw_old_group(key, part):
    shuffled = jax.random.permutation(jax.random.fold_in(key, 11), N_GROUP).astype(jnp.int32)
    task_ids = jnp.arange(TASKS, dtype=jnp.int32)
    return shuffled[task_ids % N_GROUP]


def draw_new_group(key, part):
    shuffled = jax.random.permutation(jax.random.fold_in(key, 23), N_GROUP).astype(jnp.int32)
    task_ids = jnp.arange(TASKS, dtype=jnp.int32)
    return shuffled[(task_ids + task_ids // N_GROUP) % N_GROUP]


def set_ends(values, stream_key, smallest, high):
    place = [jax.random.randint(jax.random.fold_in(stream_key, axis), (), 0, length) for axis, length in enumerate(values.shape)]
    widest = values.shape.index(max(values.shape))
    next_to = place[:widest] + [(place[widest] + 1) % values.shape[widest]] + place[widest + 1:]
    return values.at[tuple(place)].set(smallest).at[tuple(next_to)].set(high)


def level_of(rng, dims, split, smallest, high):
    def one(dim, blocks):
        heights = jax.random.uniform(jax.random.fold_in(jax.random.fold_in(rng, 6), dim), (blocks,), jnp.float32, smallest / len(split), high / len(split))
        return jnp.repeat(jnp.exp(heights), dims[dim] // blocks).reshape((-1,) + (1,) * (len(dims) - dim - 1))

    loudness = one(*split[0])
    for cut in split[1:]:
        loudness = loudness * one(*cut)
    return loudness


def bell_draw(own_key, shape, width, bound, cuts=(), kind=jnp.bfloat16):
    values = width * jax.random.normal(own_key, shape, jnp.float32)
    if cuts:
        values = values * level_of(own_key, shape, cuts, -0.22, 0.18)
    return jnp.clip(values, -bound, bound).astype(kind)


def setup_inputs(seed: int = 0) -> dict:
    seeds = jax.random.split(jax.random.key(seed), 11)
    tokens = bell_draw(seeds[0], (TOTAL_SLOTS, SAMPLE, D), 1.0, 6.0, ((0, 4), (1, 8)))
    image_keys = draw_image_keys(jax.random.fold_in(seeds[10], 71), 0)
    image_values = bell_draw(seeds[2], (TOTAL_SLOTS, IMG, HH), 3.0, 18.0, ((0, 4), (1, 8)))
    text_len = set_ends(jax.random.randint(seeds[3], (TOTAL_SLOTS,), 1, SAMPLE + 1), jax.random.fold_in(seeds[3], 1), 1, SAMPLE).astype(jnp.int32)
    image_len = set_ends(jax.random.randint(seeds[4], (TOTAL_SLOTS,), 1, IMG + 1), jax.random.fold_in(seeds[4], 1), 1, IMG).astype(jnp.int32)
    counts = draw_counts(jax.random.fold_in(seeds[10], 71), 0)
    old_group = draw_old_group(jax.random.fold_in(seeds[10], 71), 0)
    new_group = draw_new_group(jax.random.fold_in(seeds[10], 71), 0)
    w_query = bell_draw(seeds[8], (D, HH), D ** -0.5, 0.125)
    w_out = bell_draw(seeds[9], (HH, D), HH ** -0.5, 0.125)
    return dict(tokens=tokens, image_keys=image_keys, image_values=image_values, text_len=text_len, image_len=image_len, counts=counts, old_group=old_group, new_group=new_group, w_query=w_query, w_out=w_out)


masked_score = -1e+30
norm_eps = 1e-05

def layout(counts, old_group, new_group, group_count, slot_count):
    task_order = jnp.arange(counts.shape[0], dtype=jnp.int32)
    earlier = task_order[None, :] < task_order[:, None]
    same_old = old_group[None, :] == old_group[:, None]
    same_new = new_group[None, :] == new_group[:, None]
    old_start = lax.optimization_barrier(jnp.sum(jnp.where(earlier & same_old, counts[None, :], 0), axis=1)).astype(jnp.int32)
    new_start = lax.optimization_barrier(jnp.sum(jnp.where(earlier & same_new, counts[None, :], 0), axis=1)).astype(jnp.int32)
    target = jnp.arange(group_count * slot_count, dtype=jnp.int32)
    target_group = target // slot_count
    target_slot = target % slot_count
    matches = (new_group[None, :] == target_group[:, None]) & (target_slot[:, None] >= new_start[None, :]) & (target_slot[:, None] < (new_start + counts)[None, :])
    filled = jnp.any(matches, axis=1)
    offset = (target_slot - lax.optimization_barrier(jnp.sum(jnp.where(matches, new_start[None, :], 0), axis=1))).astype(jnp.int32)
    source_group = lax.optimization_barrier(jnp.sum(jnp.where(matches, old_group[None, :], 0), axis=1)).astype(jnp.int32)
    source_slot = (lax.optimization_barrier(jnp.sum(jnp.where(matches, old_start[None, :], 0), axis=1)) + offset).astype(jnp.int32)
    return (filled, source_group, source_slot, offset, old_start)

def normalize(samples_rows):
    values = samples_rows.astype(jnp.float32)
    average = lax.optimization_barrier(jnp.mean(values, axis=-1, keepdims=True))
    centred = values - average
    variance = lax.optimization_barrier(jnp.mean(centred * centred, axis=-1, keepdims=True))
    return (centred * lax.rsqrt(variance + norm_eps)).astype(jnp.bfloat16)

def reference(tokens, image_keys, image_values, text_len, image_len, counts, old_group, new_group, w_query, w_out):
    slot_count = tokens.shape[0] // N_GROUP
    score_scale = HEAD_DIM ** (-0.5)
    filled, source_group, source_slot, offset, old_start = layout(counts, old_group, new_group, N_GROUP, slot_count)

    def single_sample(inputs):
        sample_rows, key_rows, value_rows, limit_text, limit_key = inputs
        normal = normalize(sample_rows)
        queries = (jnp.dot(normal, w_query, preferred_element_type=jnp.float32) * score_scale).astype(jnp.bfloat16)
        head_queries = lax.optimization_barrier(queries).astype(jnp.float32).reshape(SAMPLE, HEADS, HEAD_DIM)
        head_keys = key_rows.astype(jnp.float32).reshape(IMG, HEADS, HEAD_DIM)
        head_values = value_rows.astype(jnp.float32).reshape(IMG, HEADS, HEAD_DIM)
        scores = jnp.einsum('qhd,khd->hqk', head_queries, head_keys)
        allowed = (jnp.arange(IMG, dtype=jnp.int32) < limit_key)[None, None, :]
        scores = jnp.where(allowed, scores, masked_score)
        row_max = lax.optimization_barrier(jnp.max(scores, axis=-1, keepdims=True))
        probs = jnp.where(allowed, jnp.exp(scores - row_max), 0.0)
        running_sum = lax.optimization_barrier(jnp.sum(probs, axis=-1))
        weights = lax.optimization_barrier(probs.astype(jnp.bfloat16)).astype(jnp.float32)
        context = jnp.einsum('hqk,khd->hqd', weights, head_values) / running_sum[..., None]
        context = context.transpose(1, 0, 2).reshape(SAMPLE, HEADS * HEAD_DIM).astype(jnp.bfloat16)
        projected = jnp.dot(context, w_out, preferred_element_type=jnp.float32)
        kept_rows = jnp.arange(SAMPLE, dtype=jnp.int32) < limit_text
        return jnp.where(kept_rows[:, None], projected, 0.0).astype(jnp.bfloat16)
    computed = lax.map(single_sample, (tokens, image_keys, image_values, text_len, image_len))
    source = jnp.where(filled, source_group * slot_count + source_slot, 0).astype(jnp.int32)
    picked = jnp.take(computed, source, axis=0)
    return jnp.where(filled[:, None, None], picked, jnp.zeros((), jnp.bfloat16))
```

```python
import functools

import jax
import jax.numpy as jnp
from jax import lax
from jax.experimental import pallas as pl
from jax.experimental.pallas import tpu as pltpu
from jax.sharding import PartitionSpec as P

HEAD_DIM = 128
PAIR = 2
HEADS_AT_ONCE = 4
OUT_TILE = 512

masked_score = -1e30
norm_eps = 1e-05


def pick_tasks(own, other, counts, group_index):
    order = jnp.arange(counts.shape[0], dtype=jnp.int32)
    earlier = (order[None, :] < order[:, None]) & (own[None, :] == own[:, None])
    start = jnp.sum(jnp.where(earlier, counts[None, :], 0), axis=1)
    rank = jnp.sum(earlier.astype(jnp.int32), axis=1)
    lanes = jnp.arange(PAIR, dtype=jnp.int32)
    mine = (own == group_index)[None, :] & (rank[None, :] == lanes[:, None])

    def chosen(values):
        return jnp.sum(jnp.where(mine, values[None, :], 0), axis=1)

    return chosen(counts), chosen(start), chosen(other)


def old_tables(counts, old_group, new_group, group_index, group_count, half):
    size, start, target = pick_tasks(old_group, new_group, counts, group_index)
    step = jnp.arange(half, dtype=jnp.int32)[:, None]
    valid = step < size[None, :]
    slot = jnp.where(valid, start[None, :] + step, 0)
    first = jnp.where(valid[:, 0], target[0], (target[1] + 1) % group_count)
    second = jnp.where(valid[:, 1], target[1], (first + 1) % group_count)
    return valid, slot, jnp.stack([first, second], axis=1)


def new_tables(counts, old_group, new_group, group_index, half):
    size, start, source = pick_tasks(new_group, old_group, counts, group_index)
    step = jnp.arange(half, dtype=jnp.int32)[:, None]
    valid = step < size[None, :]
    empty = (~valid).reshape(-1).astype(jnp.int32)
    spare = (jnp.cumsum(empty) - empty).reshape(half, PAIR) + jnp.sum(size)
    slot = jnp.where(valid, start[None, :] + step, spare)
    return valid, slot, jnp.broadcast_to(source[None, :], valid.shape)


def normalize(samples_rows):
    values = samples_rows.astype(jnp.float32)
    average = jnp.mean(values, axis=-1, keepdims=True)
    centred = values - average
    variance = jnp.mean(centred * centred, axis=-1, keepdims=True)
    return (centred * lax.rsqrt(variance + norm_eps)).astype(jnp.bfloat16)


def attend_kernel(table, q_ref, k_ref, v_ref, w_hbm, out_ref, w_ref, ctx_ref, sem):
    lane = pl.program_id(0)
    rows, width = ctx_ref.shape
    seq_count, piece = k_ref.shape[0], k_ref.shape[1]
    keys = seq_count * piece
    load = pltpu.make_async_copy(w_hbm, w_ref, sem)

    @pl.when(lane == 0)
    def _():
        load.start()

    valid = table[0, lane] > 0
    key_limit = table[3, lane]
    row_limit = table[4, lane]

    @pl.when(valid)
    def _():
        allowed = lax.broadcasted_iota(jnp.int32, (rows, keys), 1) < key_limit

        def some_heads(block, carry):
            for inner in range(HEADS_AT_ONCE):
                first = pl.multiple_of((block * HEADS_AT_ONCE + inner) * HEAD_DIM, HEAD_DIM)
                columns = pl.ds(first, HEAD_DIM)
                key = k_ref[:, :, columns].reshape(keys, HEAD_DIM)
                value = v_ref[:, :, columns].reshape(keys, HEAD_DIM)
                scores = lax.dot_general(
                    q_ref[0, :, columns],
                    key,
                    (((1,), (1,)), ((), ())),
                    preferred_element_type=jnp.float32,
                )
                scores = jnp.where(allowed, scores, masked_score)
                top = jnp.max(scores, axis=-1, keepdims=True)
                probs = jnp.where(allowed, jnp.exp(scores - top), 0.0)
                total = jnp.sum(probs, axis=-1, keepdims=True)
                context = jnp.dot(
                    probs.astype(jnp.bfloat16), value, preferred_element_type=jnp.float32
                )
                ctx_ref[:, columns] = (context / total).astype(jnp.bfloat16)
            return carry

        lax.fori_loop(0, width // (HEAD_DIM * HEADS_AT_ONCE), some_heads, 0)

    @pl.when(lane == 0)
    def _():
        load.wait()

    @pl.when(valid)
    def _():
        features = out_ref.shape[2]
        kept = lax.broadcasted_iota(jnp.int32, (rows, OUT_TILE), 0) < row_limit

        def some_columns(block, carry):
            columns = pl.ds(pl.multiple_of(block * OUT_TILE, OUT_TILE), OUT_TILE)
            projected = jnp.dot(
                ctx_ref[...], w_ref[:, columns], preferred_element_type=jnp.float32
            )
            out_ref[0, :, columns] = jnp.where(kept, projected, 0.0).astype(jnp.bfloat16)
            return carry

        lax.fori_loop(0, features // OUT_TILE, some_columns, 0)

    @pl.when(jnp.logical_not(valid))
    def _():
        out_ref[...] = jnp.zeros_like(out_ref)


def attend(table, queries, gathered, w_out, group_count):
    _, rows, width = queries.shape
    seq_count, packed, _ = gathered.shape
    piece = packed // (2 * PAIR)
    features = w_out.shape[1]
    keys = seq_count * piece
    return pl.pallas_call(
        attend_kernel,
        name="attend",
        out_shape=jax.ShapeDtypeStruct((group_count, rows, features), jnp.bfloat16),
        grid_spec=pltpu.PrefetchScalarGridSpec(
            num_scalar_prefetch=1,
            grid=(PAIR,),
            in_specs=[
                pl.BlockSpec((1, rows, width), lambda a, t: (t[1, a], 0, 0)),
                pl.BlockSpec((seq_count, piece, width), lambda a, t: (0, a, 0)),
                pl.BlockSpec((seq_count, piece, width), lambda a, t: (0, PAIR + a, 0)),
                pl.BlockSpec(memory_space=pl.ANY),
            ],
            out_specs=pl.BlockSpec((1, rows, features), lambda a, t: (t[2, a], 0, 0)),
            scratch_shapes=[
                pltpu.VMEM(w_out.shape, jnp.bfloat16),
                pltpu.VMEM((rows, width), jnp.bfloat16),
                pltpu.SemaphoreType.DMA,
            ],
        ),
        compiler_params=pltpu.CompilerParams(
            dimension_semantics=("arbitrary",), vmem_limit_bytes=40 * 1024 * 1024
        ),
        cost_estimate=pl.CostEstimate(
            flops=PAIR * 2 * rows * width * (2 * keys + features),
            bytes_accessed=2 * (w_out.size + PAIR * (2 * rows + 2 * keys) * width),
            transcendentals=PAIR * rows * keys * (width // HEAD_DIM),
        ),
    )(table, queries, gathered, gathered, w_out)


def place_kernel(table, in_ref, *rest):
    out_ref = rest[-1]
    lane = pl.program_id(0)
    valid = table[0, lane] > 0

    @pl.when(valid)
    def _():
        out_ref[...] = in_ref[...]

    @pl.when(jnp.logical_not(valid))
    def _():
        out_ref[...] = jnp.zeros_like(out_ref)


def place(table, incoming, result, slot_count):
    _, rows, features = incoming.shape
    block = (1, rows, features)
    earlier = () if result is None else (result,)
    return pl.pallas_call(
        place_kernel,
        name="place",
        out_shape=jax.ShapeDtypeStruct((slot_count, rows, features), jnp.bfloat16),
        grid_spec=pltpu.PrefetchScalarGridSpec(
            num_scalar_prefetch=1,
            grid=(PAIR,),
            in_specs=[pl.BlockSpec(block, lambda a, t: (t[2, a], 0, 0))]
            + [pl.BlockSpec(memory_space=pl.ANY)] * len(earlier),
            out_specs=pl.BlockSpec(block, lambda a, t: (t[1, a], 0, 0)),
        ),
        input_output_aliases={2: 0} if earlier else {},
        compiler_params=pltpu.CompilerParams(dimension_semantics=("arbitrary",)),
        cost_estimate=pl.CostEstimate(
            flops=0, bytes_accessed=4 * PAIR * rows * features, transcendentals=0
        ),
    )(table, incoming, *earlier)


def on_device(
    tokens,
    image_keys,
    image_values,
    text_len,
    image_len,
    counts,
    old_group,
    new_group,
    w_query,
    w_out,
):
    group_count = lax.axis_size("group")
    slot_count, row_count, features = tokens.shape
    half = slot_count // PAIR
    piece = image_keys.shape[1]
    width = w_query.shape[1]
    group_index = lax.axis_index("group")
    first_row = lax.axis_index("seq") * row_count
    own_first = group_index * slot_count
    text_limit = lax.dynamic_slice_in_dim(text_len, own_first, slot_count) - first_row
    key_limit = lax.dynamic_slice_in_dim(image_len, own_first, slot_count)

    old_valid, old_slot, old_target = old_tables(
        counts, old_group, new_group, group_index, group_count, half
    )
    new_valid, new_slot, new_source = new_tables(counts, old_group, new_group, group_index, half)
    old_table = jnp.stack(
        [
            old_valid.astype(jnp.int32),
            old_slot,
            old_target,
            jnp.take(key_limit, old_slot),
            jnp.take(text_limit, old_slot),
        ],
        axis=1,
    )
    new_table = jnp.stack([new_valid.astype(jnp.int32), new_slot, new_source], axis=1)

    gathered = []
    for step in range(half):
        pieces = [
            lax.dynamic_index_in_dim(rows, old_slot[step, lane], 0, keepdims=False)
            for rows in (image_keys, image_values)
            for lane in range(PAIR)
        ]
        packed = jnp.concatenate(pieces, axis=0)
        gathered.append(lax.all_gather(packed, "seq", axis=0, tiled=False))

    normal = normalize(tokens).reshape(slot_count * row_count, features)
    queries = (
        jnp.dot(normal, w_query, preferred_element_type=jnp.float32) * HEAD_DIM ** (-0.5)
    ).astype(jnp.bfloat16)
    queries = queries.reshape(slot_count, row_count, width)

    result = None
    for step in range(half):
        outgoing = attend(old_table[step], queries, gathered[step], w_out, group_count)
        incoming = lax.all_to_all(outgoing, "group", split_axis=0, concat_axis=0, tiled=True)
        result = place(new_table[step], incoming, result, slot_count)
    return result


def solution(mesh):
    rows = P("group", "seq", None)
    return jax.shard_map(
        on_device,
        mesh=mesh,
        in_specs=(rows, rows, rows) + (P(),) * 7,
        out_specs=rows,
        check_vma=False,
    )
```

```python
import functools

import jax
import jax.numpy as jnp
from jax import lax
from jax.experimental import pallas as pl
from jax.experimental.pallas import tpu as pltpu
from jax.sharding import PartitionSpec as P

HEAD_DIM = 128
PAIR = 2
HEADS_AT_ONCE = 4
OUT_TILE = 512

masked_score = -1e30
norm_eps = 1e-05


OLD_VALID, OLD_SLOT, OLD_TARGET, OLD_KEYS, OLD_ROWS = range(5)
NEW_VALID, NEW_SLOT, NEW_SOURCE, NEW_KEYS, NEW_ROWS = range(5, 10)
FIELDS = 10


def at(step, field, lane):
    return (step * FIELDS + field) * PAIR + lane


def table_kernel(slot_count, row_count, group_count, counts, old, new, text, image, out):
    task_count = counts.shape[0]
    half = slot_count // PAIR
    group = lax.axis_index("group")
    first_row = lax.axis_index("seq") * row_count
    size = [counts[t] for t in range(task_count)]
    olds = [old[t] for t in range(task_count)]
    news = [new[t] for t in range(task_count)]
    zero = jnp.int32(0)

    def starts_and_ranks(own):
        starts, ranks = [], []
        for t in range(task_count):
            start, rank = zero, zero
            for u in range(t):
                same = own[u] == own[t]
                start = start + jnp.where(same, size[u], 0)
                rank = rank + jnp.where(same, 1, 0)
            starts.append(start)
            ranks.append(rank)
        return starts, ranks

    old_start, old_rank = starts_and_ranks(olds)
    new_start, new_rank = starts_and_ranks(news)

    def lanes(own, ranks, values):
        found = []
        for lane in range(PAIR):
            value = zero
            for t in range(task_count):
                hit = jnp.logical_and(own[t] == group, ranks[t] == lane)
                value = jnp.where(hit, values[t], value)
            found.append(value)
        return found

    old_size = lanes(olds, old_rank, size)
    old_first = lanes(olds, old_rank, old_start)
    target = lanes(olds, old_rank, news)
    new_size = lanes(news, new_rank, size)
    new_first = lanes(news, new_rank, new_start)
    source = lanes(news, new_rank, olds)
    source_first = lanes(news, new_rank, old_start)
    spare = new_size[0] + new_size[1]
    for step in range(half):
        valid = [step < old_size[lane] for lane in range(PAIR)]
        after = lax.rem(target[1] + 1, group_count)
        first = jnp.where(valid[0], target[0], after)
        second = jnp.where(valid[1], target[1], lax.rem(first + 1, group_count))
        for lane in range(PAIR):
            slot = jnp.where(valid[lane], old_first[lane] + step, 0)
            out[at(step, OLD_VALID, lane)] = jnp.where(valid[lane], 1, 0)
            out[at(step, OLD_SLOT, lane)] = slot
            out[at(step, OLD_TARGET, lane)] = (first, second)[lane]
            out[at(step, OLD_KEYS, lane)] = image[group * slot_count + slot]
            out[at(step, OLD_ROWS, lane)] = text[group * slot_count + slot] - first_row
            here = step < new_size[lane]
            came = source[lane] * slot_count + jnp.where(here, source_first[lane] + step, 0)
            out[at(step, NEW_VALID, lane)] = jnp.where(here, 1, 0)
            out[at(step, NEW_SLOT, lane)] = jnp.where(here, new_first[lane] + step, spare)
            out[at(step, NEW_SOURCE, lane)] = source[lane]
            out[at(step, NEW_KEYS, lane)] = image[came]
            out[at(step, NEW_ROWS, lane)] = text[came] - first_row
            spare = spare + jnp.where(here, 0, 1)


def make_table(slot_count, row_count, group_count, *scalars):
    smem = pl.BlockSpec(memory_space=pltpu.SMEM)
    return pl.pallas_call(
        functools.partial(table_kernel, slot_count, row_count, group_count),
        name="table",
        out_shape=jax.ShapeDtypeStruct((slot_count * FIELDS,), jnp.int32),
        in_specs=[smem] * len(scalars),
        out_specs=smem,
    )(*scalars)


def pack_kernel(table, *refs):
    out_ref = refs[-1]
    first = 0
    for ref in refs[:-1]:
        out_ref[0, first : first + ref.shape[1]] = ref[0]
        first += ref.shape[1]


def pack(table, slot_of, count, *arrays):
    rows = sum(array.shape[1] for array in arrays)
    width = arrays[0].shape[2]
    return pl.pallas_call(
        pack_kernel,
        name="pack",
        out_shape=jax.ShapeDtypeStruct((count, rows, width), arrays[0].dtype),
        grid_spec=pltpu.PrefetchScalarGridSpec(
            num_scalar_prefetch=1,
            grid=(count,),
            in_specs=[
                pl.BlockSpec((1,) + array.shape[1:], lambda i, t: (slot_of(i, t), 0, 0))
                for array in arrays
            ],
            out_specs=pl.BlockSpec((1, rows, width), lambda i, t: (i, 0, 0)),
        ),
        cost_estimate=pl.CostEstimate(
            flops=0, bytes_accessed=4 * count * rows * width, transcendentals=0
        ),
    )(table, *arrays)


def unpack_kernel(table, in_ref, normal_ref, packed_ref):
    rows = normal_ref.shape[1]
    tile = min(rows, 64)
    for first in range(0, rows, tile):
        normal_ref[0, first : first + tile] = normalize(in_ref[0, first : first + tile])
    packed_ref[0] = in_ref[0, rows:]


def unpack(table, step, incoming, rows):
    _, height, width = incoming.shape
    return pl.pallas_call(
        unpack_kernel,
        name="unpack",
        out_shape=(
            jax.ShapeDtypeStruct((PAIR, rows, width), incoming.dtype),
            jax.ShapeDtypeStruct((PAIR, height - rows, width), incoming.dtype),
        ),
        grid_spec=pltpu.PrefetchScalarGridSpec(
            num_scalar_prefetch=1,
            grid=(PAIR,),
            in_specs=[
                pl.BlockSpec(
                    (1, height, width), lambda a, t: (t[at(step, NEW_SOURCE, a)], 0, 0)
                )
            ],
            out_specs=(
                pl.BlockSpec((1, rows, width), lambda a, t: (a, 0, 0)),
                pl.BlockSpec((1, height - rows, width), lambda a, t: (a, 0, 0)),
            ),
        ),
        cost_estimate=pl.CostEstimate(
            flops=8 * PAIR * rows * width,
            bytes_accessed=4 * PAIR * height * width,
            transcendentals=0,
        ),
    )(table, incoming)


def normalize(samples_rows):
    values = samples_rows.astype(jnp.float32)
    average = jnp.mean(values, axis=-1, keepdims=True)
    centred = values - average
    variance = jnp.mean(centred * centred, axis=-1, keepdims=True)
    return (centred * lax.rsqrt(variance + norm_eps)).astype(jnp.bfloat16)


def attend_kernel(fields, table, q_ref, k_ref, v_ref, w_hbm, *rest):
    out_ref, w_ref, ctx_ref, sem = rest[-4:]
    lane = pl.program_id(0)
    rows, width = ctx_ref.shape
    seq_count, piece = k_ref.shape[0], k_ref.shape[1]
    keys = seq_count * piece
    load = pltpu.make_async_copy(w_hbm, w_ref, sem)

    @pl.when(lane == 0)
    def _():
        load.start()

    valid = table[fields[0] + lane] > 0
    key_limit = table[fields[1] + lane]
    row_limit = table[fields[2] + lane]

    @pl.when(valid)
    def _():
        allowed = lax.broadcasted_iota(jnp.int32, (rows, keys), 1) < key_limit

        def some_heads(block, carry):
            for inner in range(HEADS_AT_ONCE):
                first = pl.multiple_of((block * HEADS_AT_ONCE + inner) * HEAD_DIM, HEAD_DIM)
                columns = pl.ds(first, HEAD_DIM)
                key = k_ref[:, :, columns].reshape(keys, HEAD_DIM)
                value = v_ref[:, :, columns].reshape(keys, HEAD_DIM)
                scores = lax.dot_general(
                    q_ref[0, :, columns],
                    key,
                    (((1,), (1,)), ((), ())),
                    preferred_element_type=jnp.float32,
                )
                scores = jnp.where(allowed, scores, masked_score)
                top = jnp.max(scores, axis=-1, keepdims=True)
                probs = jnp.where(allowed, jnp.exp(scores - top), 0.0)
                total = jnp.sum(probs, axis=-1, keepdims=True)
                context = jnp.dot(
                    probs.astype(jnp.bfloat16), value, preferred_element_type=jnp.float32
                )
                ctx_ref[:, columns] = (context / total).astype(jnp.bfloat16)
            return carry

        lax.fori_loop(0, width // (HEAD_DIM * HEADS_AT_ONCE), some_heads, 0)

    @pl.when(lane == 0)
    def _():
        load.wait()

    @pl.when(valid)
    def _():
        features = out_ref.shape[2]
        kept = lax.broadcasted_iota(jnp.int32, (rows, OUT_TILE), 0) < row_limit

        def some_columns(block, carry):
            columns = pl.ds(pl.multiple_of(block * OUT_TILE, OUT_TILE), OUT_TILE)
            projected = jnp.dot(
                ctx_ref[...], w_ref[:, columns], preferred_element_type=jnp.float32
            )
            out_ref[0, :, columns] = jnp.where(kept, projected, 0.0).astype(jnp.bfloat16)
            return carry

        lax.fori_loop(0, features // OUT_TILE, some_columns, 0)

    @pl.when(jnp.logical_not(valid))
    def _():
        out_ref[...] = jnp.zeros_like(out_ref)


def attend(table, step, queries, gathered, w_out, out_count, result=None):
    _, rows, width = queries.shape
    seq_count, packed, _ = gathered.shape
    piece = packed // (2 * PAIR)
    features = w_out.shape[1]
    keys = seq_count * piece
    if result is None:
        names, to = (OLD_VALID, OLD_KEYS, OLD_ROWS), OLD_TARGET
        earlier = ()

        def query_of(a, t):
            return t[at(step, OLD_SLOT, a)], 0, 0
    else:
        names, to = (NEW_VALID, NEW_KEYS, NEW_ROWS), NEW_SLOT
        earlier = (result,)

        def query_of(a, t):
            return a, 0, 0

    fields = tuple(at(step, name, 0) for name in names)
    return pl.pallas_call(
        functools.partial(attend_kernel, fields),
        name="attend",
        out_shape=jax.ShapeDtypeStruct((out_count, rows, features), jnp.bfloat16),
        grid_spec=pltpu.PrefetchScalarGridSpec(
            num_scalar_prefetch=1,
            grid=(PAIR,),
            in_specs=[
                pl.BlockSpec((1, rows, width), query_of),
                pl.BlockSpec((seq_count, piece, width), lambda a, t: (0, 2 * a, 0)),
                pl.BlockSpec((seq_count, piece, width), lambda a, t: (0, 2 * a + 1, 0)),
                pl.BlockSpec(memory_space=pl.ANY),
            ]
            + [pl.BlockSpec(memory_space=pl.ANY)] * len(earlier),
            out_specs=pl.BlockSpec(
                (1, rows, features), lambda a, t: (t[at(step, to, a)], 0, 0)
            ),
            scratch_shapes=[
                pltpu.VMEM(w_out.shape, jnp.bfloat16),
                pltpu.VMEM((rows, width), jnp.bfloat16),
                pltpu.SemaphoreType.DMA,
            ],
        ),
        input_output_aliases={5: 0} if earlier else {},
        compiler_params=pltpu.CompilerParams(
            dimension_semantics=("arbitrary",), vmem_limit_bytes=40 * 1024 * 1024
        ),
        cost_estimate=pl.CostEstimate(
            flops=PAIR * 2 * rows * width * (2 * keys + features),
            bytes_accessed=2 * (w_out.size + PAIR * (2 * rows + 2 * keys) * width),
            transcendentals=PAIR * rows * keys * (width // HEAD_DIM),
        ),
    )(table, queries, gathered, gathered, w_out, *earlier)


def place_kernel(field, table, in_ref, *rest):
    out_ref = rest[-1]
    lane = pl.program_id(0)
    valid = table[field + lane] > 0

    @pl.when(valid)
    def _():
        out_ref[...] = in_ref[...]

    @pl.when(jnp.logical_not(valid))
    def _():
        out_ref[...] = jnp.zeros_like(out_ref)


def place(table, step, incoming, result, slot_count):
    _, rows, features = incoming.shape
    block = (1, rows, features)
    earlier = () if result is None else (result,)
    return pl.pallas_call(
        functools.partial(place_kernel, at(step, NEW_VALID, 0)),
        name="place",
        out_shape=jax.ShapeDtypeStruct((slot_count, rows, features), jnp.bfloat16),
        grid_spec=pltpu.PrefetchScalarGridSpec(
            num_scalar_prefetch=1,
            grid=(PAIR,),
            in_specs=[pl.BlockSpec(block, lambda a, t: (t[at(step, NEW_SOURCE, a)], 0, 0))]
            + [pl.BlockSpec(memory_space=pl.ANY)] * len(earlier),
            out_specs=pl.BlockSpec(block, lambda a, t: (t[at(step, NEW_SLOT, a)], 0, 0)),
        ),
        input_output_aliases={2: 0} if earlier else {},
        compiler_params=pltpu.CompilerParams(dimension_semantics=("arbitrary",)),
        cost_estimate=pl.CostEstimate(
            flops=0, bytes_accessed=4 * PAIR * rows * features, transcendentals=0
        ),
    )(table, incoming, *earlier)


def on_device(
    tokens,
    image_keys,
    image_values,
    text_len,
    image_len,
    counts,
    old_group,
    new_group,
    w_query,
    w_out,
):
    group_count = lax.axis_size("group")
    slot_count, row_count, features = tokens.shape
    half = slot_count // PAIR
    width = w_query.shape[1]
    table = make_table(
        slot_count, row_count, group_count, counts, old_group, new_group, text_len, image_len
    )

    def exchange(blocks):
        return lax.all_to_all(blocks, "group", split_axis=0, concat_axis=0, tiled=True)

    def gather(packed):
        return lax.all_gather(packed.reshape(-1, width), "seq", axis=0, tiled=False)

    def project(normal):
        flat = normal.reshape(-1, features)
        queries = jnp.dot(flat, w_query, preferred_element_type=jnp.float32)
        queries = (queries * HEAD_DIM ** (-0.5)).astype(jnp.bfloat16)
        return queries.reshape(normal.shape[0], row_count, width)

    gathered = {}
    for step in range(1, half):

        def slot_of(lane, t, step=step):
            return t[at(step, OLD_SLOT, lane)]

        gathered[step] = gather(pack(table, slot_of, PAIR, image_keys, image_values))

    def slot_to(group, t):
        to_first = t[at(0, OLD_TARGET, 0)] == group
        return jnp.where(to_first, t[at(0, OLD_SLOT, 0)], t[at(0, OLD_SLOT, 1)])

    moved = exchange(pack(table, slot_to, group_count, tokens, image_keys, image_values))
    queries = project(normalize(tokens))

    result = None
    for step in range(1, half):
        outgoing = attend(table, step, queries, gathered[step], w_out, group_count)
        incoming = exchange(outgoing)
        if step == half - 1:
            normal, packed = unpack(table, 0, moved, row_count)
            result = attend(
                table, 0, project(normal), gather(packed), w_out, slot_count, result
            )
        result = place(table, step, incoming, result, slot_count)
    return result


def solution(mesh):
    rows = P("group", "seq", None)
    return jax.shard_map(
        on_device,
        mesh=mesh,
        in_specs=(rows, rows, rows) + (P(),) * 7,
        out_specs=rows,
        check_vma=False,
    )
```

```python
import functools

import jax
import jax.numpy as jnp
from jax import lax
from jax.experimental import pallas as pl
from jax.experimental.pallas import tpu as pltpu
from jax.sharding import PartitionSpec as P


HEAD_DIM = 128
PAIR = 2
HEADS_AT_ONCE = 4
OUT_TILE = 512

masked_score = -1e30
norm_eps = 1e-05


OLD_VALID, OLD_SLOT, OLD_TARGET, OLD_KEYS, OLD_ROWS = range(5)
NEW_VALID, NEW_SLOT, NEW_SOURCE, NEW_KEYS, NEW_ROWS = range(5, 10)
FIELDS = 10


def at(step, field, lane):
    return (step * FIELDS + field) * PAIR + lane


def table_kernel(slot_count, row_count, counts, old, new, text, image, out):
    task_count = counts.shape[0]
    half = slot_count // PAIR
    group = lax.axis_index("group")
    first_row = lax.axis_index("seq") * row_count
    size = [counts[t] for t in range(task_count)]
    olds = [old[t] for t in range(task_count)]
    news = [new[t] for t in range(task_count)]
    zero = jnp.int32(0)

    def starts_and_ranks(own):
        starts, ranks = [], []
        for t in range(task_count):
            start, rank = zero, zero
            for u in range(t):
                same = own[u] == own[t]
                start = start + jnp.where(same, size[u], 0)
                rank = rank + jnp.where(same, 1, 0)
            starts.append(start)
            ranks.append(rank)
        return starts, ranks

    old_start, old_rank = starts_and_ranks(olds)
    new_start, new_rank = starts_and_ranks(news)

    def lanes(own, ranks, values):
        found = []
        for lane in range(PAIR):
            value = zero
            for t in range(task_count):
                hit = jnp.logical_and(own[t] == group, ranks[t] == lane)
                value = jnp.where(hit, values[t], value)
            found.append(value)
        return found

    old_size = lanes(olds, old_rank, size)
    old_first = lanes(olds, old_rank, old_start)
    target = lanes(olds, old_rank, news)
    new_size = lanes(news, new_rank, size)
    new_first = lanes(news, new_rank, new_start)
    source = lanes(news, new_rank, olds)
    source_first = lanes(news, new_rank, old_start)
    spare = new_size[0] + new_size[1]
    for step in range(half):
        valid = [step < old_size[lane] for lane in range(PAIR)]
        for lane in range(PAIR):
            slot = jnp.where(valid[lane], old_first[lane] + step, 0)
            out[at(step, OLD_VALID, lane)] = jnp.where(valid[lane], 1, 0)
            out[at(step, OLD_SLOT, lane)] = slot
            out[at(step, OLD_TARGET, lane)] = target[lane] ^ group
            out[at(step, OLD_KEYS, lane)] = image[group * slot_count + slot]
            out[at(step, OLD_ROWS, lane)] = text[group * slot_count + slot] - first_row
            here = step < new_size[lane]
            came = source[lane] * slot_count + jnp.where(here, source_first[lane] + step, 0)
            out[at(step, NEW_VALID, lane)] = jnp.where(here, 1, 0)
            out[at(step, NEW_SLOT, lane)] = jnp.where(here, new_first[lane] + step, spare)
            out[at(step, NEW_SOURCE, lane)] = source[lane] ^ group
            out[at(step, NEW_KEYS, lane)] = image[came]
            out[at(step, NEW_ROWS, lane)] = text[came] - first_row
            spare = spare + jnp.where(here, 0, 1)


def make_table(slot_count, row_count, *scalars):
    smem = pl.BlockSpec(memory_space=pltpu.SMEM)
    return pl.pallas_call(
        functools.partial(table_kernel, slot_count, row_count),
        name="table",
        out_shape=jax.ShapeDtypeStruct((slot_count * FIELDS,), jnp.int32),
        in_specs=[smem] * len(scalars),
        out_specs=smem,
    )(*scalars)


def pack_kernel(table, *refs):
    out_ref = refs[-1]
    first = 0
    for ref in refs[:-1]:
        out_ref[0, first : first + ref.shape[1]] = ref[0]
        first += ref.shape[1]


def pack(table, slot_of, count, *arrays):
    rows = sum(array.shape[1] for array in arrays)
    width = arrays[0].shape[2]
    return pl.pallas_call(
        pack_kernel,
        name="pack",
        out_shape=jax.ShapeDtypeStruct((count, rows, width), arrays[0].dtype),
        grid_spec=pltpu.PrefetchScalarGridSpec(
            num_scalar_prefetch=1,
            grid=(count,),
            in_specs=[
                pl.BlockSpec((1,) + array.shape[1:], lambda i, t: (slot_of(i, t), 0, 0))
                for array in arrays
            ],
            out_specs=pl.BlockSpec((1, rows, width), lambda i, t: (i, 0, 0)),
        ),
        cost_estimate=pl.CostEstimate(
            flops=0, bytes_accessed=4 * count * rows * width, transcendentals=0
        ),
    )(table, *arrays)


def spread_kernel(array_count, table, *refs):
    for place, out_ref in enumerate(refs[array_count:]):

        @pl.when(pl.program_id(0) == place)
        def _(out_ref=out_ref):
            first = 0
            for ref in refs[:array_count]:
                out_ref[first : first + ref.shape[1]] = ref[0]
                first += ref.shape[1]


def spread(table, slot_of, count, *arrays):
    rows = sum(array.shape[1] for array in arrays)
    width = arrays[0].shape[2]
    return pl.pallas_call(
        functools.partial(spread_kernel, len(arrays)),
        name="spread",
        out_shape=[jax.ShapeDtypeStruct((rows, width), arrays[0].dtype)] * count,
        grid_spec=pltpu.PrefetchScalarGridSpec(
            num_scalar_prefetch=1,
            grid=(count,),
            in_specs=[
                pl.BlockSpec((1,) + array.shape[1:], lambda i, t: (slot_of(i, t), 0, 0))
                for array in arrays
            ],
            out_specs=[pl.BlockSpec((rows, width), lambda i, t: (0, 0))] * count,
        ),
        cost_estimate=pl.CostEstimate(
            flops=0, bytes_accessed=4 * count * rows * width, transcendentals=0
        ),
    )(table, *arrays)


def unpack_kernel(field, count, table, *refs):
    normal_ref, packed_ref, in_ref = refs[count:]
    source = table[field + pl.program_id(0)]
    for place in range(count):

        @pl.when(source == place)
        def _(ref=refs[place]):
            in_ref[0] = ref[...]

    rows = normal_ref.shape[1]
    tile = min(rows, 64)
    for first in range(0, rows, tile):
        normal_ref[0, first : first + tile] = normalize(in_ref[0, first : first + tile])
    packed_ref[0] = in_ref[0, rows:]


def unpack(table, step, incoming, rows):
    height, width = incoming[0].shape
    dtype = incoming[0].dtype
    return pl.pallas_call(
        functools.partial(unpack_kernel, at(step, NEW_SOURCE, 0), len(incoming)),
        name="unpack",
        out_shape=(
            jax.ShapeDtypeStruct((PAIR, rows, width), dtype),
            jax.ShapeDtypeStruct((PAIR, height - rows, width), dtype),
        ),
        grid_spec=pltpu.PrefetchScalarGridSpec(
            num_scalar_prefetch=1,
            grid=(PAIR,),
            in_specs=[pl.BlockSpec((height, width), lambda a, t: (0, 0))] * len(incoming),
            out_specs=(
                pl.BlockSpec((1, rows, width), lambda a, t: (a, 0, 0)),
                pl.BlockSpec((1, height - rows, width), lambda a, t: (a, 0, 0)),
            ),
            scratch_shapes=[pltpu.VMEM((1, height, width), dtype)],
        ),
        cost_estimate=pl.CostEstimate(
            flops=8 * PAIR * rows * width,
            bytes_accessed=4 * PAIR * height * width,
            transcendentals=0,
        ),
    )(table, *incoming)


def normalize(samples_rows):
    values = samples_rows.astype(jnp.float32)
    average = jnp.mean(values, axis=-1, keepdims=True)
    centred = values - average
    variance = jnp.mean(centred * centred, axis=-1, keepdims=True)
    return (centred * lax.rsqrt(variance + norm_eps)).astype(jnp.bfloat16)


def attend_kernel(fields, out_count, table, q_ref, k_ref, v_ref, w_hbm, *rest):
    w_ref, ctx_ref, done_ref, sem = rest[-4:]
    outs = rest[-4 - out_count : -4]
    out_ref = done_ref if out_count > 1 else outs[0]
    lane = pl.program_id(0)
    rows, width = ctx_ref.shape
    seq_count, piece = k_ref.shape[0], k_ref.shape[1]
    keys = seq_count * piece
    load = pltpu.make_async_copy(w_hbm, w_ref, sem)

    @pl.when(lane == 0)
    def _():
        load.start()

    valid = table[fields[0] + lane] > 0
    key_limit = table[fields[1] + lane]
    row_limit = table[fields[2] + lane]

    @pl.when(valid)
    def _():
        allowed = lax.broadcasted_iota(jnp.int32, (rows, keys), 1) < key_limit

        def some_heads(block, carry):
            for inner in range(HEADS_AT_ONCE):
                first = pl.multiple_of((block * HEADS_AT_ONCE + inner) * HEAD_DIM, HEAD_DIM)
                columns = pl.ds(first, HEAD_DIM)
                key = k_ref[:, :, columns].reshape(keys, HEAD_DIM)
                value = v_ref[:, :, columns].reshape(keys, HEAD_DIM)
                scores = lax.dot_general(
                    q_ref[0, :, columns],
                    key,
                    (((1,), (1,)), ((), ())),
                    preferred_element_type=jnp.float32,
                )
                scores = jnp.where(allowed, scores, masked_score)
                top = jnp.max(scores, axis=-1, keepdims=True)
                probs = jnp.where(allowed, jnp.exp(scores - top), 0.0)
                total = jnp.sum(probs, axis=-1, keepdims=True)
                context = jnp.dot(
                    probs.astype(jnp.bfloat16), value, preferred_element_type=jnp.float32
                )
                ctx_ref[:, columns] = (context / total).astype(jnp.bfloat16)
            return carry

        lax.fori_loop(0, width // (HEAD_DIM * HEADS_AT_ONCE), some_heads, 0)

    @pl.when(lane == 0)
    def _():
        load.wait()

    @pl.when(valid)
    def _():
        features = out_ref.shape[2]
        kept = lax.broadcasted_iota(jnp.int32, (rows, OUT_TILE), 0) < row_limit

        def some_columns(block, carry):
            columns = pl.ds(pl.multiple_of(block * OUT_TILE, OUT_TILE), OUT_TILE)
            projected = jnp.dot(
                ctx_ref[...], w_ref[:, columns], preferred_element_type=jnp.float32
            )
            out_ref[0, :, columns] = jnp.where(kept, projected, 0.0).astype(jnp.bfloat16)
            return carry

        lax.fori_loop(0, features // OUT_TILE, some_columns, 0)

    for place in range(out_count if out_count > 1 else 0):

        @pl.when(jnp.logical_and(valid, table[fields[3] + lane] == place))
        def _(ref=outs[place]):
            ref[...] = done_ref[0]

    if out_count == 1:

        @pl.when(jnp.logical_not(valid))
        def _():
            out_ref[...] = jnp.zeros_like(out_ref)


def attend(table, step, queries, gathered, w_out, group_count, result=None):
    _, rows, width = queries.shape
    seq_count, packed, _ = gathered.shape
    piece = packed // (2 * PAIR)
    features = w_out.shape[1]
    keys = seq_count * piece
    if result is None:
        names = (OLD_VALID, OLD_KEYS, OLD_ROWS, OLD_TARGET)
        earlier = ()
        out_shape = [jax.ShapeDtypeStruct((rows, features), jnp.bfloat16)] * group_count
        out_specs = [pl.BlockSpec((rows, features), lambda a, t: (0, 0))] * group_count

        def query_of(a, t):
            return t[at(step, OLD_SLOT, a)], 0, 0
    else:
        names = (NEW_VALID, NEW_KEYS, NEW_ROWS)
        earlier = (result,)
        out_shape = [jax.ShapeDtypeStruct(result.shape, jnp.bfloat16)]
        out_specs = [
            pl.BlockSpec((1, rows, features), lambda a, t: (t[at(step, NEW_SLOT, a)], 0, 0))
        ]

        def query_of(a, t):
            return a, 0, 0

    fields = tuple(at(step, name, 0) for name in names)
    return pl.pallas_call(
        functools.partial(attend_kernel, fields, len(out_shape)),
        name="attend",
        out_shape=out_shape,
        grid_spec=pltpu.PrefetchScalarGridSpec(
            num_scalar_prefetch=1,
            grid=(PAIR,),
            in_specs=[
                pl.BlockSpec((1, rows, width), query_of),
                pl.BlockSpec((seq_count, piece, width), lambda a, t: (0, 2 * a, 0)),
                pl.BlockSpec((seq_count, piece, width), lambda a, t: (0, 2 * a + 1, 0)),
                pl.BlockSpec(memory_space=pl.ANY),
            ]
            + [pl.BlockSpec(memory_space=pl.ANY)] * len(earlier),
            out_specs=out_specs,
            scratch_shapes=[
                pltpu.VMEM(w_out.shape, jnp.bfloat16),
                pltpu.VMEM((rows, width), jnp.bfloat16),
                pltpu.VMEM((1, rows, features), jnp.bfloat16),
                pltpu.SemaphoreType.DMA,
            ],
        ),
        input_output_aliases={5: 0} if earlier else {},
        compiler_params=pltpu.CompilerParams(
            dimension_semantics=("arbitrary",), vmem_limit_bytes=40 * 1024 * 1024
        ),
        cost_estimate=pl.CostEstimate(
            flops=PAIR * 2 * rows * width * (2 * keys + features),
            bytes_accessed=2 * (w_out.size + PAIR * (2 * rows + 2 * keys) * width),
            transcendentals=PAIR * rows * keys * (width // HEAD_DIM),
        ),
    )(table, queries, gathered, gathered, w_out, *earlier)


def place_kernel(field, source_field, count, table, *refs):
    out_ref = refs[-1]
    lane = pl.program_id(0)
    valid = table[field + lane] > 0
    for place in range(count):

        @pl.when(jnp.logical_and(valid, table[source_field + lane] == place))
        def _(ref=refs[place]):
            out_ref[0] = ref[...]

    @pl.when(jnp.logical_not(valid))
    def _():
        out_ref[...] = jnp.zeros_like(out_ref)


def place(table, step, incoming, result, slot_count):
    rows, features = incoming[0].shape
    block = (1, rows, features)
    count = len(incoming)
    earlier = () if result is None else (result,)
    return pl.pallas_call(
        functools.partial(
            place_kernel, at(step, NEW_VALID, 0), at(step, NEW_SOURCE, 0), count
        ),
        name="place",
        out_shape=jax.ShapeDtypeStruct((slot_count, rows, features), jnp.bfloat16),
        grid_spec=pltpu.PrefetchScalarGridSpec(
            num_scalar_prefetch=1,
            grid=(PAIR,),
            in_specs=[pl.BlockSpec((rows, features), lambda a, t: (0, 0))] * count
            + [pl.BlockSpec(memory_space=pl.ANY)] * len(earlier),
            out_specs=pl.BlockSpec(block, lambda a, t: (t[at(step, NEW_SLOT, a)], 0, 0)),
        ),
        input_output_aliases={1 + count: 0} if earlier else {},
        compiler_params=pltpu.CompilerParams(dimension_semantics=("arbitrary",)),
        cost_estimate=pl.CostEstimate(
            flops=0, bytes_accessed=4 * PAIR * rows * features, transcendentals=0
        ),
    )(table, *incoming, *earlier)


def on_device(
    tokens,
    image_keys,
    image_values,
    text_len,
    image_len,
    counts,
    old_group,
    new_group,
    w_query,
    w_out,
):
    group_count = lax.axis_size("group")
    slot_count, row_count, features = tokens.shape
    half = slot_count // PAIR
    width = w_query.shape[1]
    table = make_table(
        slot_count, row_count, counts, old_group, new_group, text_len, image_len
    )

    def exchange(blocks):
        received = [blocks[0]]
        for apart in range(1, group_count):
            pairs = [(here, here ^ apart) for here in range(group_count)]
            received.append(lax.ppermute(blocks[apart], "group", pairs))
        return received

    def gather(packed):
        return lax.all_gather(packed.reshape(-1, width), "seq", axis=0, tiled=False)

    def project(normal):
        flat = normal.reshape(-1, features)
        queries = jnp.dot(flat, w_query, preferred_element_type=jnp.float32)
        queries = (queries * HEAD_DIM ** (-0.5)).astype(jnp.bfloat16)
        return queries.reshape(normal.shape[0], row_count, width)

    gathered = {}
    for step in range(1, half):

        def slot_of(lane, t, step=step):
            return t[at(step, OLD_SLOT, lane)]

        gathered[step] = gather(pack(table, slot_of, PAIR, image_keys, image_values))

    def slot_to(apart, t):
        to_first = t[at(0, OLD_TARGET, 0)] == apart
        return jnp.where(to_first, t[at(0, OLD_SLOT, 0)], t[at(0, OLD_SLOT, 1)])

    moved = exchange(spread(table, slot_to, group_count, tokens, image_keys, image_values))
    queries = project(normalize(tokens))

    result = None
    for step in range(1, half):
        outgoing = attend(table, step, queries, gathered[step], w_out, group_count)
        incoming = exchange(outgoing)
        if step == 1:
            moved, _ = lax.optimization_barrier((moved, outgoing[0]))
        if step == half - 1:
            normal, packed = unpack(table, 0, moved, row_count)
            result = attend(
                table, 0, project(normal), gather(packed), w_out, group_count, result
            )[0]
        result = place(table, step, incoming, result, slot_count)
    return result


def solution(mesh):
    rows = P("group", "seq", None)
    return jax.shard_map(
        on_device,
        mesh=mesh,
        in_specs=(rows, rows, rows) + (P(),) * 7,
        out_specs=rows,
        check_vma=False,
    )
```

```python
import functools

import jax
import jax.numpy as jnp
from jax import lax
from jax.experimental import pallas as pl
from jax.experimental.pallas import tpu as pltpu
from jax.sharding import PartitionSpec as P


HEAD_DIM = 128
PAIR = 2
HEADS_AT_ONCE = 4
OUT_TILE = 512

masked_score = -1e30
norm_eps = 1e-05


OLD_VALID, OLD_SLOT, OLD_TARGET, OLD_KEYS, OLD_ROWS = range(5)
NEW_VALID, NEW_SLOT, NEW_SOURCE, NEW_KEYS, NEW_ROWS = range(5, 10)
FIELDS = 10


def at(step, field, lane):
    return (step * FIELDS + field) * PAIR + lane


def table_kernel(slot_count, row_count, counts, old, new, text, image, out):
    task_count = counts.shape[0]
    half = slot_count // PAIR
    group = lax.axis_index("group")
    first_row = lax.axis_index("seq") * row_count
    size = [counts[t] for t in range(task_count)]
    olds = [old[t] for t in range(task_count)]
    news = [new[t] for t in range(task_count)]
    zero = jnp.int32(0)

    def starts_and_ranks(own):
        starts, ranks = [], []
        for t in range(task_count):
            start, rank = zero, zero
            for u in range(t):
                same = own[u] == own[t]
                start = start + jnp.where(same, size[u], 0)
                rank = rank + jnp.where(same, 1, 0)
            starts.append(start)
            ranks.append(rank)
        return starts, ranks

    old_start, old_rank = starts_and_ranks(olds)
    new_start, new_rank = starts_and_ranks(news)

    def lanes(own, ranks, values):
        found = []
        for lane in range(PAIR):
            value = zero
            for t in range(task_count):
                hit = jnp.logical_and(own[t] == group, ranks[t] == lane)
                value = jnp.where(hit, values[t], value)
            found.append(value)
        return found

    old_size = lanes(olds, old_rank, size)
    old_first = lanes(olds, old_rank, old_start)
    target = lanes(olds, old_rank, news)
    new_size = lanes(news, new_rank, size)
    new_first = lanes(news, new_rank, new_start)
    source = lanes(news, new_rank, olds)
    source_first = lanes(news, new_rank, old_start)
    spare = new_size[0] + new_size[1]
    for step in range(half):
        valid = [step < old_size[lane] for lane in range(PAIR)]
        for lane in range(PAIR):
            slot = jnp.where(valid[lane], old_first[lane] + step, 0)
            out[at(step, OLD_VALID, lane)] = jnp.where(valid[lane], 1, 0)
            out[at(step, OLD_SLOT, lane)] = slot
            out[at(step, OLD_TARGET, lane)] = target[lane] ^ group
            out[at(step, OLD_KEYS, lane)] = image[group * slot_count + slot]
            out[at(step, OLD_ROWS, lane)] = text[group * slot_count + slot] - first_row
            here = step < new_size[lane]
            came = source[lane] * slot_count + jnp.where(here, source_first[lane] + step, 0)
            out[at(step, NEW_VALID, lane)] = jnp.where(here, 1, 0)
            out[at(step, NEW_SLOT, lane)] = jnp.where(here, new_first[lane] + step, spare)
            out[at(step, NEW_SOURCE, lane)] = source[lane] ^ group
            out[at(step, NEW_KEYS, lane)] = image[came]
            out[at(step, NEW_ROWS, lane)] = text[came] - first_row
            spare = spare + jnp.where(here, 0, 1)


def make_table(slot_count, row_count, *scalars):
    smem = pl.BlockSpec(memory_space=pltpu.SMEM)
    return pl.pallas_call(
        functools.partial(table_kernel, slot_count, row_count),
        name="table",
        out_shape=jax.ShapeDtypeStruct((slot_count * FIELDS,), jnp.int32),
        in_specs=[smem] * len(scalars),
        out_specs=smem,
    )(*scalars)


def pack_kernel(table, *refs):
    out_ref = refs[-1]
    first = 0
    for ref in refs[:-1]:
        out_ref[0, first : first + ref.shape[1]] = ref[0]
        first += ref.shape[1]


def pack(table, slot_of, count, *arrays):
    rows = sum(array.shape[1] for array in arrays)
    width = arrays[0].shape[2]
    return pl.pallas_call(
        pack_kernel,
        name="pack",
        out_shape=jax.ShapeDtypeStruct((count, rows, width), arrays[0].dtype),
        grid_spec=pltpu.PrefetchScalarGridSpec(
            num_scalar_prefetch=1,
            grid=(count,),
            in_specs=[
                pl.BlockSpec((1,) + array.shape[1:], lambda i, t: (slot_of(i, t), 0, 0))
                for array in arrays
            ],
            out_specs=pl.BlockSpec((1, rows, width), lambda i, t: (i, 0, 0)),
        ),
        cost_estimate=pl.CostEstimate(
            flops=0, bytes_accessed=4 * count * rows * width, transcendentals=0
        ),
    )(table, *arrays)


def spread_kernel(array_count, table, *refs):
    for place, out_ref in enumerate(refs[array_count:]):

        @pl.when(pl.program_id(0) == place)
        def _(out_ref=out_ref):
            first = 0
            for ref in refs[:array_count]:
                out_ref[first : first + ref.shape[1]] = ref[0]
                first += ref.shape[1]


def spread(table, slot_of, count, *arrays):
    rows = sum(array.shape[1] for array in arrays)
    width = arrays[0].shape[2]
    return pl.pallas_call(
        functools.partial(spread_kernel, len(arrays)),
        name="spread",
        out_shape=[jax.ShapeDtypeStruct((rows, width), arrays[0].dtype)] * count,
        grid_spec=pltpu.PrefetchScalarGridSpec(
            num_scalar_prefetch=1,
            grid=(count,),
            in_specs=[
                pl.BlockSpec((1,) + array.shape[1:], lambda i, t: (slot_of(i, t), 0, 0))
                for array in arrays
            ],
            out_specs=[pl.BlockSpec((rows, width), lambda i, t: (0, 0))] * count,
        ),
        cost_estimate=pl.CostEstimate(
            flops=0, bytes_accessed=4 * count * rows * width, transcendentals=0
        ),
    )(table, *arrays)


def unpack_kernel(field, change, table, *refs):
    out_ref = refs[-1]
    source = table[field + pl.program_id(0)]
    for place, ref in enumerate(refs[:-1]):

        @pl.when(source == place)
        def _(ref=ref):
            rows = ref.shape[0]
            tile = min(rows, 64)
            for first in range(0, rows, tile):
                out_ref[0, first : first + tile] = change(ref[first : first + tile])


def unpack(table, step, incoming, first, rows, change):
    width = incoming[0].shape[1]
    block = first // rows
    return pl.pallas_call(
        functools.partial(unpack_kernel, at(step, NEW_SOURCE, 0), change),
        name="unpack",
        out_shape=jax.ShapeDtypeStruct((PAIR, rows, width), incoming[0].dtype),
        grid_spec=pltpu.PrefetchScalarGridSpec(
            num_scalar_prefetch=1,
            grid=(PAIR,),
            in_specs=[pl.BlockSpec((rows, width), lambda a, t: (block, 0))] * len(incoming),
            out_specs=pl.BlockSpec((1, rows, width), lambda a, t: (a, 0, 0)),
        ),
        cost_estimate=pl.CostEstimate(
            flops=8 * PAIR * rows * width,
            bytes_accessed=4 * PAIR * rows * width,
            transcendentals=0,
        ),
    )(table, *incoming)


def normalize(samples_rows):
    values = samples_rows.astype(jnp.float32)
    average = jnp.mean(values, axis=-1, keepdims=True)
    centred = values - average
    variance = jnp.mean(centred * centred, axis=-1, keepdims=True)
    return (centred * lax.rsqrt(variance + norm_eps)).astype(jnp.bfloat16)


def attend_kernel(fields, out_count, table, q_ref, k_ref, v_ref, w_hbm, *rest):
    w_ref, ctx_ref, done_ref, sem = rest[-4:]
    outs = rest[-4 - out_count : -4]
    out_ref = done_ref if out_count > 1 else outs[0]
    lane = pl.program_id(0)
    rows, width = ctx_ref.shape
    seq_count, piece = k_ref.shape[0], k_ref.shape[1]
    keys = seq_count * piece
    load = pltpu.make_async_copy(w_hbm, w_ref, sem)

    @pl.when(lane == 0)
    def _():
        load.start()

    valid = table[fields[0] + lane] > 0
    key_limit = table[fields[1] + lane]
    row_limit = table[fields[2] + lane]

    @pl.when(valid)
    def _():
        allowed = lax.broadcasted_iota(jnp.int32, (rows, keys), 1) < key_limit

        def some_heads(block, carry):
            for inner in range(HEADS_AT_ONCE):
                first = pl.multiple_of((block * HEADS_AT_ONCE + inner) * HEAD_DIM, HEAD_DIM)
                columns = pl.ds(first, HEAD_DIM)
                key = k_ref[:, :, columns].reshape(keys, HEAD_DIM)
                value = v_ref[:, :, columns].reshape(keys, HEAD_DIM)
                scores = lax.dot_general(
                    q_ref[0, :, columns],
                    key,
                    (((1,), (1,)), ((), ())),
                    preferred_element_type=jnp.float32,
                )
                scores = jnp.where(allowed, scores, masked_score)
                top = jnp.max(scores, axis=-1, keepdims=True)
                probs = jnp.where(allowed, jnp.exp(scores - top), 0.0)
                total = jnp.sum(probs, axis=-1, keepdims=True)
                context = jnp.dot(
                    probs.astype(jnp.bfloat16), value, preferred_element_type=jnp.float32
                )
                ctx_ref[:, columns] = (context / total).astype(jnp.bfloat16)
            return carry

        lax.fori_loop(0, width // (HEAD_DIM * HEADS_AT_ONCE), some_heads, 0)

    @pl.when(lane == 0)
    def _():
        load.wait()

    @pl.when(valid)
    def _():
        features = out_ref.shape[2]
        kept = lax.broadcasted_iota(jnp.int32, (rows, OUT_TILE), 0) < row_limit

        def some_columns(block, carry):
            columns = pl.ds(pl.multiple_of(block * OUT_TILE, OUT_TILE), OUT_TILE)
            projected = jnp.dot(
                ctx_ref[...], w_ref[:, columns], preferred_element_type=jnp.float32
            )
            out_ref[0, :, columns] = jnp.where(kept, projected, 0.0).astype(jnp.bfloat16)
            return carry

        lax.fori_loop(0, features // OUT_TILE, some_columns, 0)

    for place in range(out_count if out_count > 1 else 0):

        @pl.when(jnp.logical_and(valid, table[fields[3] + lane] == place))
        def _(ref=outs[place]):
            ref[...] = done_ref[0]

    if out_count == 1:

        @pl.when(jnp.logical_not(valid))
        def _():
            out_ref[...] = jnp.zeros_like(out_ref)


def attend(table, step, queries, gathered, w_out, group_count, result=None):
    _, rows, width = queries.shape
    seq_count, packed, _ = gathered.shape
    piece = packed // (2 * PAIR)
    features = w_out.shape[1]
    keys = seq_count * piece
    if result is None:
        names = (OLD_VALID, OLD_KEYS, OLD_ROWS, OLD_TARGET)
        earlier = ()
        out_shape = [jax.ShapeDtypeStruct((rows, features), jnp.bfloat16)] * group_count
        out_specs = [pl.BlockSpec((rows, features), lambda a, t: (0, 0))] * group_count

        def query_of(a, t):
            return t[at(step, OLD_SLOT, a)], 0, 0
    else:
        names = (NEW_VALID, NEW_KEYS, NEW_ROWS)
        earlier = (result,)
        out_shape = [jax.ShapeDtypeStruct(result.shape, jnp.bfloat16)]
        out_specs = [
            pl.BlockSpec((1, rows, features), lambda a, t: (t[at(step, NEW_SLOT, a)], 0, 0))
        ]

        def query_of(a, t):
            return a, 0, 0

    fields = tuple(at(step, name, 0) for name in names)
    return pl.pallas_call(
        functools.partial(attend_kernel, fields, len(out_shape)),
        name="attend",
        out_shape=out_shape,
        grid_spec=pltpu.PrefetchScalarGridSpec(
            num_scalar_prefetch=1,
            grid=(PAIR,),
            in_specs=[
                pl.BlockSpec((1, rows, width), query_of),
                pl.BlockSpec((seq_count, piece, width), lambda a, t: (0, 2 * a, 0)),
                pl.BlockSpec((seq_count, piece, width), lambda a, t: (0, 2 * a + 1, 0)),
                pl.BlockSpec(memory_space=pl.ANY),
            ]
            + [pl.BlockSpec(memory_space=pl.ANY)] * len(earlier),
            out_specs=out_specs,
            scratch_shapes=[
                pltpu.VMEM(w_out.shape, jnp.bfloat16),
                pltpu.VMEM((rows, width), jnp.bfloat16),
                pltpu.VMEM((1, rows, features), jnp.bfloat16),
                pltpu.SemaphoreType.DMA,
            ],
        ),
        input_output_aliases={5: 0} if earlier else {},
        compiler_params=pltpu.CompilerParams(
            dimension_semantics=("arbitrary",), vmem_limit_bytes=40 * 1024 * 1024
        ),
        cost_estimate=pl.CostEstimate(
            flops=PAIR * 2 * rows * width * (2 * keys + features),
            bytes_accessed=2 * (w_out.size + PAIR * (2 * rows + 2 * keys) * width),
            transcendentals=PAIR * rows * keys * (width // HEAD_DIM),
        ),
    )(table, queries, gathered, gathered, w_out, *earlier)


def place_kernel(field, source_field, count, table, *refs):
    out_ref = refs[-1]
    lane = pl.program_id(0)
    valid = table[field + lane] > 0
    for place in range(count):

        @pl.when(jnp.logical_and(valid, table[source_field + lane] == place))
        def _(ref=refs[place]):
            out_ref[0] = ref[...]

    @pl.when(jnp.logical_not(valid))
    def _():
        out_ref[...] = jnp.zeros_like(out_ref)


def place(table, step, incoming, result, slot_count):
    rows, features = incoming[0].shape
    block = (1, rows, features)
    count = len(incoming)
    earlier = () if result is None else (result,)
    return pl.pallas_call(
        functools.partial(
            place_kernel, at(step, NEW_VALID, 0), at(step, NEW_SOURCE, 0), count
        ),
        name="place",
        out_shape=jax.ShapeDtypeStruct((slot_count, rows, features), jnp.bfloat16),
        grid_spec=pltpu.PrefetchScalarGridSpec(
            num_scalar_prefetch=1,
            grid=(PAIR,),
            in_specs=[pl.BlockSpec((rows, features), lambda a, t: (0, 0))] * count
            + [pl.BlockSpec(memory_space=pl.ANY)] * len(earlier),
            out_specs=pl.BlockSpec(block, lambda a, t: (t[at(step, NEW_SLOT, a)], 0, 0)),
        ),
        input_output_aliases={1 + count: 0} if earlier else {},
        compiler_params=pltpu.CompilerParams(dimension_semantics=("arbitrary",)),
        cost_estimate=pl.CostEstimate(
            flops=0, bytes_accessed=4 * PAIR * rows * features, transcendentals=0
        ),
    )(table, *incoming, *earlier)


def on_device(
    tokens,
    image_keys,
    image_values,
    text_len,
    image_len,
    counts,
    old_group,
    new_group,
    w_query,
    w_out,
):
    group_count = lax.axis_size("group")
    slot_count, row_count, features = tokens.shape
    half = slot_count // PAIR
    width = w_query.shape[1]
    table = make_table(
        slot_count, row_count, counts, old_group, new_group, text_len, image_len
    )

    def exchange(blocks):
        received = [blocks[0]]
        for apart in range(1, group_count):
            pairs = [(here, here ^ apart) for here in range(group_count)]
            received.append(lax.ppermute(blocks[apart], "group", pairs))
        return received

    def gather(packed):
        return lax.all_gather(packed.reshape(-1, width), "seq", axis=0, tiled=False)

    def project(normal):
        flat = normal.reshape(-1, features)
        queries = jnp.dot(flat, w_query, preferred_element_type=jnp.float32)
        queries = (queries * HEAD_DIM ** (-0.5)).astype(jnp.bfloat16)
        return queries.reshape(normal.shape[0], row_count, width)

    gathered = {}
    for step in range(1, half):

        def slot_of(lane, t, step=step):
            return t[at(step, OLD_SLOT, lane)]

        gathered[step] = gather(pack(table, slot_of, PAIR, image_keys, image_values))

    def slot_to(apart, t):
        to_first = t[at(0, OLD_TARGET, 0)] == apart
        return jnp.where(to_first, t[at(0, OLD_SLOT, 0)], t[at(0, OLD_SLOT, 1)])

    moved = exchange(spread(table, slot_to, group_count, tokens, image_keys, image_values))
    queries = project(normalize(tokens))

    result = None
    for step in range(1, half):
        outgoing = attend(table, step, queries, gathered[step], w_out, group_count)
        incoming = exchange(outgoing)
        if step == 1:
            moved, _ = lax.optimization_barrier((moved, outgoing[0]))
        if step == half - 1:
            packed_rows = moved[0].shape[0] - row_count
            packed = unpack(table, 0, moved, row_count, packed_rows, lambda rows: rows)
            normal = unpack(table, 0, moved, 0, row_count, normalize)
            result = attend(
                table, 0, project(normal), gather(packed), w_out, group_count, result
            )[0]
        result = place(table, step, incoming, result, slot_count)
    return result


def solution(mesh):
    rows = P("group", "seq", None)
    return jax.shard_map(
        on_device,
        mesh=mesh,
        in_specs=(rows, rows, rows) + (P(),) * 7,
        out_specs=rows,
        check_vma=False,
    )
```
